512 devices in a mesh: side: 2 (over y_hi), dp: 16 (over y_lo, x, core), grp: 16 (over z).
Axes of the slice: x: 4, y: 4 (y_hi: 2, y_lo: 2; y = y_hi * 2 + y_lo), z: 16, core: 2. Of those that a mesh axis runs over, the one named last changes fastest.
Arguments:
- attn_inputs: bfloat16 [2, 2, 32768, 2048], P('side', None, ('dp', 'grp')), may hold values from -120 to 120
- token_weight: float32 [32768], P(('dp', 'grp')), may hold values from 0.05 to 37.5
- enc_lens: int32 [16, 8], P('dp'), may hold values from 1 to 5, 16 in all within a row
- dec_lens: int32 [16, 8], P('dp'), may hold values from 1 to 5, 16 in all within a row
Outputs:
- attn_results: bfloat16 [2, 2, 32768, 2048], P('side', None, ('dp', 'grp'))
The draws below stay inside these ranges and needn't reach their ends.
Inputs may be any that keep to these rules, and one draw needn't show every extreme that they name: `enc_lens`: row p lists, in pack order, how many blocks of 128 tokens the encoder part of each of pack p's 8 sequences takes; each row sums to 16 and its largest entry is exactly 5. `dec_lens`: row p lists the decoder blocks of the same 8 sequences in the same order; each row sums to 16 and its largest entry is exactly 5.
All inputs are finite; a program needn't handle non-finite values.
Results may differ from the reference program's by a relative error of at most 0.02.
Values may be sent and summed in bfloat16 or wider, within the bound.
No kernel may reach another device: no remote copies, remote signals or barrier semaphores. Data moves between devices by JAX's collectives and lax.ppermute only.
A program may use at most 64 MiB of HBM per device.

```python
import math
import jax
import jax.numpy as jnp
import numpy as np
from jax import lax

HD = 64
BLOCK = 128
NB = 16
PACK_TOK = 2048
TOKENS = 32768
SEQS = 8
MOST = 5
INNER = 2048
N_DP = 16


def draw_attn_inputs(key, part):
    keys = jax.random.split(key, 2)
    shape = (2, 2, TOKENS, INNER)
    base = jnp.clip(jax.random.normal(keys[0], shape, jnp.float32), -6.0, 6.0)
    low_attn, high_attn, low_other, high_other = (0.5, 1.6, 0.5, 2.0)
    low = jnp.array([[low_attn, low_other], [low_attn, low_other]], jnp.float32)[:, :, None, None]
    high = jnp.array([[high_attn, high_other], [high_attn, high_other]], jnp.float32)[:, :, None, None]
    spread = jax.random.uniform(keys[1], (2, 2, TOKENS, 1), jnp.float32)
    row_scale = jnp.exp(jnp.log(low) + spread * (jnp.log(high) - jnp.log(low)))
    values_all = base * row_scale
    return values_all.astype(jnp.bfloat16)


def draw_token_weight(key, part):
    keys = jax.random.split(key, 2)
    pack_count = TOKENS // PACK_TOK
    pack_index = (jnp.arange(TOKENS) // PACK_TOK).astype(jnp.int32)
    rising = 1.0 + 2.0 * pack_index.astype(jnp.float32) / max(pack_count - 1, 1)
    pack_factor = jnp.exp(jax.random.uniform(keys[1], (pack_count,), jnp.float32, math.log(0.2), math.log(5.0)))
    pack_scale = jnp.take(pack_factor, pack_index, axis=0)
    weights = jnp.exp(jax.random.uniform(keys[0], (TOKENS,), jnp.float32, math.log(0.5), math.log(2.0)))
    return (rising * pack_scale * weights).astype(jnp.float32)


def length_profile(number_of, total, limit, skew):
    portions = [(1 << 20) // math.isqrt(standing ** skew) + 1 for standing in range(2, number_of + 1)]
    rest, given = total - limit - (number_of - 1), [1] * (number_of - 1)
    while rest > 0:
        movable = [i for i in range(number_of - 1) if given[i] < limit]
        mass, remaining = sum([portions[i] for i in movable]), rest
        for i in movable:
            addition = min(limit - given[i], max(1, remaining * portions[i] // mass), rest)
            given[i] = given[i] + addition
            rest = rest - addition
    return np.array([limit] + given)


def uneven(stream_key, amount, total, bound, slope):
    if amount == 2:
        one = jax.random.randint(stream_key, (), max(1, total - bound), min(bound, total - 1) + 1)
        return jnp.stack([one, total - one])
    sizes = jnp.asarray(length_profile(amount, total, bound, slope), jnp.int32)
    couples = (amount - 1) // 2
    source_of, taker = sizes[1:1 + 2 * couples:2], sizes[2:2 + 2 * couples:2]
    margin = jnp.minimum(source_of - 1, bound - taker)
    moved = jax.random.randint(jax.random.fold_in(stream_key, 1), (couples,), 0, 1 << 20) % (margin + 1)
    sizes = sizes.at[1:1 + 2 * couples:2].set(source_of - moved).at[2:2 + 2 * couples:2].set(taker + moved)
    return sizes[jax.random.permutation(jax.random.fold_in(stream_key, 2), amount)]


def setup_inputs(seed: int = 0) -> dict:
    streams_of = jax.random.split(jax.random.key(seed), 5)
    return {
        "attn_inputs": draw_attn_inputs(jax.random.fold_in(streams_of[4], 71), 0),
        "token_weight": draw_token_weight(jax.random.fold_in(streams_of[4], 71), 0),
        "enc_lens": jax.vmap(lambda own: uneven(own, SEQS, NB, MOST, 2))(jax.random.split(streams_of[2], N_DP)).reshape((N_DP, SEQS)).astype(jnp.int32),
        "dec_lens": jax.vmap(lambda own: uneven(own, SEQS, NB, MOST, 2))(jax.random.split(streams_of[3], N_DP)).reshape((N_DP, SEQS)).astype(jnp.int32),
    }


def segment_of(blocks, block_ends):
    return lax.optimization_barrier(jnp.sum((blocks[..., None] >= block_ends).astype(jnp.int32), axis=-1))

def windows(row_lens, col_lens, block_count, window_blocks):
    row_ends = jnp.cumsum(row_lens).astype(jnp.int32)
    col_ends = jnp.cumsum(col_lens).astype(jnp.int32)
    col_starts = col_ends - col_lens.astype(jnp.int32)
    blocks = jnp.arange(block_count, dtype=jnp.int32)
    row_seg = segment_of(blocks, row_ends)
    seq_count = col_starts.shape[0]
    matched = row_seg[:, None] == jnp.arange(seq_count, dtype=jnp.int32)[None, :]
    first_block = lax.optimization_barrier(jnp.sum(jnp.where(matched, col_starts[None, :], 0), axis=1)).astype(jnp.int32)
    first_block = jnp.minimum(first_block, block_count - window_blocks)
    picks = (first_block[:, None] + jnp.arange(window_blocks, dtype=jnp.int32)[None, :]).astype(jnp.int32)
    allowed = segment_of(picks, col_ends) == row_seg[:, None]
    return (picks, allowed)

def query_pass(queries, cotangent, keys_in, values_in, picks, allowed, with_grad):
    block_count = queries.shape[0] // BLOCK
    feature_count = queries.shape[1]
    head_count = feature_count // HD
    window_rows = picks.shape[1] * BLOCK
    score_scale = 1.0 / math.sqrt(HD)
    query_blocks = queries.reshape(block_count, BLOCK, head_count, HD)
    cot_blocks = cotangent.reshape(block_count, BLOCK, head_count, HD)
    key_blocks = keys_in.reshape(block_count, BLOCK, feature_count)
    value_blocks = values_in.reshape(block_count, BLOCK, feature_count)

    def one_group(group_index):
        first_block = group_index * 4
        query_now = lax.dynamic_slice_in_dim(query_blocks, first_block, 4, 0).astype(jnp.float32)
        cot_now = lax.dynamic_slice_in_dim(cot_blocks, first_block, 4, 0).astype(jnp.float32)
        picked = lax.dynamic_slice_in_dim(picks, first_block, 4, 0).reshape(-1)
        allowed_now = lax.dynamic_slice_in_dim(allowed, first_block, 4, 0)
        key_window = jnp.take(key_blocks, picked, axis=0).reshape(4, window_rows, head_count, HD).astype(jnp.float32)
        value_window = jnp.take(value_blocks, picked, axis=0).reshape(4, window_rows, head_count, HD).astype(jnp.float32)
        key_mask = jnp.repeat(allowed_now, BLOCK, axis=1)[:, None, None, :]
        scores = jnp.einsum('gqhd,gkhd->ghqk', query_now, key_window) * score_scale
        scores = jnp.where(key_mask, scores, -jnp.inf)
        row_max = lax.optimization_barrier(jnp.max(scores, axis=-1, keepdims=True))
        log_total = row_max + jnp.log(lax.optimization_barrier(jnp.sum(jnp.exp(scores - row_max), axis=-1, keepdims=True)))
        probs = jnp.exp(scores - log_total)
        probs_b = probs.astype(jnp.bfloat16)
        attended = jnp.einsum('ghqk,gkhd->gqhd', probs_b.astype(jnp.float32), value_window).astype(jnp.bfloat16)
        row_dot = jnp.transpose(lax.optimization_barrier(jnp.sum(cot_now * attended.astype(jnp.float32), axis=-1)), (0, 2, 1))
        if with_grad:
            dprobs = jnp.einsum('gqhd,gkhd->ghqk', cot_now, value_window)
            dscores = (probs * (dprobs - row_dot[..., None]) * score_scale).astype(jnp.bfloat16)
            query_grad = jnp.einsum('ghqk,gkhd->gqhd', dscores.astype(jnp.float32), key_window).astype(jnp.bfloat16)
        else:
            query_grad = attended
        return (attended, query_grad, log_total[..., 0], row_dot)
    attended, query_grad, log_total, row_dot = lax.map(one_group, jnp.arange(block_count // 4, dtype=jnp.int32))
    attended = attended.reshape(block_count * BLOCK, feature_count)
    query_grad = query_grad.reshape(block_count * BLOCK, feature_count)
    log_total = log_total.reshape(block_count, head_count, BLOCK)
    row_dot = row_dot.reshape(block_count, head_count, BLOCK)
    return (attended, query_grad, log_total, row_dot)

def key_pass(queries, cotangent, keys_in, values_in, log_total, row_dot, picks, allowed):
    block_count = queries.shape[0] // BLOCK
    feature_count = queries.shape[1]
    head_count = feature_count // HD
    window_blocks = picks.shape[1]
    window_rows = window_blocks * BLOCK
    score_scale = 1.0 / math.sqrt(HD)
    query_blocks = queries.reshape(block_count, BLOCK, feature_count)
    cot_blocks = cotangent.reshape(block_count, BLOCK, feature_count)
    key_blocks = keys_in.reshape(block_count, BLOCK, head_count, HD)
    value_blocks = values_in.reshape(block_count, BLOCK, head_count, HD)

    def one_group(group_index):
        first_block = group_index * 4
        key_now = lax.dynamic_slice_in_dim(key_blocks, first_block, 4, 0).astype(jnp.float32)
        value_now = lax.dynamic_slice_in_dim(value_blocks, first_block, 4, 0).astype(jnp.float32)
        picked = lax.dynamic_slice_in_dim(picks, first_block, 4, 0).reshape(-1)
        allowed_now = lax.dynamic_slice_in_dim(allowed, first_block, 4, 0)
        query_window = jnp.take(query_blocks, picked, axis=0).reshape(4, window_rows, head_count, HD).astype(jnp.float32)
        cot_window = jnp.take(cot_blocks, picked, axis=0).reshape(4, window_rows, head_count, HD).astype(jnp.float32)
        total_window = jnp.take(log_total, picked, axis=0).reshape(4, window_blocks, head_count, BLOCK)
        total_window = jnp.transpose(total_window, (0, 2, 1, 3)).reshape(4, head_count, window_rows)
        dot_window = jnp.take(row_dot, picked, axis=0).reshape(4, window_blocks, head_count, BLOCK)
        dot_window = jnp.transpose(dot_window, (0, 2, 1, 3)).reshape(4, head_count, window_rows)
        query_mask = jnp.repeat(allowed_now, BLOCK, axis=1)[:, None, :, None]
        scores = jnp.einsum('gqhd,gkhd->ghqk', query_window, key_now) * score_scale
        scores = jnp.where(query_mask, scores, -jnp.inf)
        probs = jnp.exp(scores - total_window[..., None])
        probs_b = probs.astype(jnp.bfloat16)
        value_grad = jnp.einsum('ghqk,gqhd->gkhd', probs_b.astype(jnp.float32), cot_window).astype(jnp.bfloat16)
        dprobs = jnp.einsum('gqhd,gkhd->ghqk', cot_window, value_now)
        dscores = (probs * (dprobs - dot_window[..., None]) * score_scale).astype(jnp.bfloat16)
        key_grad = jnp.einsum('ghqk,gqhd->gkhd', dscores.astype(jnp.float32), query_window).astype(jnp.bfloat16)
        return (key_grad, value_grad)
    key_grad, value_grad = lax.map(one_group, jnp.arange(block_count // 4, dtype=jnp.int32))
    return (key_grad.reshape(block_count * BLOCK, feature_count), value_grad.reshape(block_count * BLOCK, feature_count))

def reference(attn_inputs, token_weight, enc_lens, dec_lens):
    weight_sum = jnp.sum(token_weight)
    factor = TOKENS / weight_sum
    pack_count = TOKENS // PACK_TOK

    def one_pack(pack_index):
        start_row = pack_index * PACK_TOK
        pack_slice = lax.dynamic_slice_in_dim(attn_inputs, start_row, PACK_TOK, 2)
        weight_slice = lax.dynamic_slice_in_dim(token_weight, start_row, PACK_TOK, 0)
        cotangent = (pack_slice[1, 1].astype(jnp.float32) * (weight_slice * factor)[:, None]).astype(jnp.bfloat16)
        enc_row = lax.dynamic_index_in_dim(enc_lens, pack_index, 0, keepdims=False)
        dec_row = lax.dynamic_index_in_dim(dec_lens, pack_index, 0, keepdims=False)
        dec_picks, dec_allowed = windows(dec_row, enc_row, NB, MOST)
        enc_picks, enc_allowed = windows(enc_row, dec_row, NB, MOST)
        attended, query_grad, log_total, row_dot = query_pass(pack_slice[1, 0], cotangent, pack_slice[0, 0], pack_slice[0, 1], dec_picks, dec_allowed, True)
        key_grad, value_grad = key_pass(pack_slice[1, 0], cotangent, pack_slice[0, 0], pack_slice[0, 1], log_total, row_dot, enc_picks, enc_allowed)
        return jnp.stack([jnp.stack([key_grad, value_grad]), jnp.stack([attended, query_grad])])
    pack_parts = lax.map(one_pack, jnp.arange(pack_count, dtype=jnp.int32))
    return jnp.transpose(pack_parts, (1, 2, 0, 3, 4)).reshape(2, 2, TOKENS, INNER)
```

```python
import functools
import math

import jax
import jax.numpy as jnp
from jax import lax
from jax.experimental import pallas as pl
from jax.experimental.pallas import tpu as pltpu
from jax.sharding import Mesh
from jax.sharding import PartitionSpec as P

HD = 64
BLOCK = 128
MOST = 5
LANES = 2 * HD
DP_GRP = ("dp_0", "dp_1", "dp_2", "grp")
DP = ("dp_0", "dp_1", "dp_2")
HEADS = ("side", "grp")
EXP2_SCALE = math.log2(math.e) / math.sqrt(HD)


def over_axes(value, axes):
    for axis in axes:
        value = lax.psum(value, axis)
    return value


def low_lanes(shape):
    return lax.broadcasted_iota(jnp.int32, shape, len(shape) - 1) < HD


def pack_kernel(scale_ref, rows_ref, out_ref):
    pair_count = rows_ref.shape[2] // LANES
    scale = jnp.broadcast_to(scale_ref[...], (BLOCK, LANES))
    for pair in range(pair_count):
        cols = slice(pair * LANES, (pair + 1) * LANES)
        first = rows_ref[0, :, cols]
        second = (rows_ref[1, :, cols].astype(jnp.float32) * scale).astype(jnp.bfloat16)
        out_ref[2 * pair] = jnp.concatenate([first[:, :HD], second[:, :HD]], axis=1)
        out_ref[2 * pair + 1] = jnp.concatenate([first[:, HD:], second[:, HD:]], axis=1)


def unpack_kernel(coef_ref, side_ref, heads_ref, out_ref):
    pair_count = out_ref.shape[2] // LANES
    side = side_ref[0]
    coef = jnp.where(low_lanes((BLOCK, LANES)), coef_ref[0], coef_ref[1])
    for pair in range(pair_count):
        cols = slice(pair * LANES, (pair + 1) * LANES)
        one = (heads_ref[2 * pair].astype(jnp.float32) * coef).astype(jnp.bfloat16)
        two = (heads_ref[2 * pair + 1].astype(jnp.float32) * coef).astype(jnp.bfloat16)
        out_ref[side, :, cols] = jnp.concatenate([one[:, :HD], two[:, :HD]], axis=1)
        out_ref[1 - side, :, cols] = jnp.concatenate([one[:, HD:], two[:, HD:]], axis=1)


def attention_kernel(start_ref, count_ref, rows_ref, out_ref, total_ref):
    token_count = rows_ref.shape[0] // 2
    block_count = token_count // BLOCK
    total_ref[...] = jnp.zeros_like(total_ref)

    def block_with(window, dec_row, enc_row):
        query = rows_ref[pl.ds(dec_row, BLOCK), :]
        low = low_lanes(query.shape)
        zero = jnp.zeros_like(query)
        split = jnp.concatenate(
            [jnp.where(low, query, zero), jnp.where(low, zero, query)], axis=0
        )
        keys = rows_ref[pl.ds(enc_row, window * BLOCK), :]
        both = lax.dot_general(
            keys, split, (((1,), (1,)), ((), ())), preferred_element_type=jnp.float32
        )
        scores = both[:, :BLOCK] * EXP2_SCALE
        dprobs = both[:, BLOCK:]
        raw = jnp.exp2(scores - jnp.max(scores, axis=0, keepdims=True))
        probs = raw * (1.0 / jnp.sum(raw, axis=0, keepdims=True))
        row_dot = jnp.sum(probs * dprobs, axis=0, keepdims=True)
        dscores = probs * (dprobs - row_dot)
        pair = jnp.concatenate(
            [dscores.astype(jnp.bfloat16), probs.astype(jnp.bfloat16)], axis=1
        )
        total_ref[pl.ds(enc_row, window * BLOCK), :] += jnp.dot(
            pair, split, preferred_element_type=jnp.float32
        )
        mixed = lax.dot_general(
            pair, keys, (((0,), (0,)), ((), ())), preferred_element_type=jnp.float32
        )
        out_ref[pl.ds(dec_row, BLOCK), :] = jnp.where(
            low, mixed[:BLOCK], mixed[BLOCK:]
        ).astype(jnp.bfloat16)

    def step(block, carry):
        dec_row = pl.multiple_of(token_count + block * BLOCK, BLOCK)
        enc_row = pl.multiple_of(start_ref[block] * BLOCK, BLOCK)
        for window in range(1, MOST + 1):

            @pl.when(count_ref[block] == window)
            def _():
                block_with(window, dec_row, enc_row)

        return carry

    lax.fori_loop(0, block_count, step, 0)
    out_ref[pl.ds(0, token_count), :] = total_ref[...].astype(jnp.bfloat16)


def encoder_ranges(enc_row, dec_row, block_count):
    enc_ends = jnp.cumsum(enc_row)
    dec_ends = jnp.cumsum(dec_row)
    blocks = jnp.arange(block_count, dtype=jnp.int32)
    inside = (blocks[:, None] >= (dec_ends - dec_row)[None, :]) & (
        blocks[:, None] < dec_ends[None, :]
    )
    starts = jnp.sum(jnp.where(inside, (enc_ends - enc_row)[None, :], 0), axis=1)
    counts = jnp.sum(jnp.where(inside, enc_row[None, :], 0), axis=1)
    return starts.astype(jnp.int32), counts.astype(jnp.int32)


VMEM = pl.BlockSpec(memory_space=pltpu.VMEM)
SMEM = pl.BlockSpec(memory_space=pltpu.SMEM)


def per_device(attn_inputs, token_weight, enc_lens, dec_lens):
    local_rows = attn_inputs[0]
    slots, row_count, feature_count = local_rows.shape
    head_count = feature_count // HD
    block_count = head_count // 2
    side = lax.axis_index("side")
    scale = jnp.where(side == 1, token_weight, 1.0)[:, None]
    packed = pl.pallas_call(
        pack_kernel,
        out_shape=jax.ShapeDtypeStruct((head_count, row_count, LANES), jnp.bfloat16),
        in_specs=[VMEM, VMEM],
        out_specs=VMEM,
        name="pack",
    )(scale, local_rows)
    arrived = lax.all_to_all(packed, HEADS, split_axis=0, concat_axis=0, tiled=True)
    starts, counts = encoder_ranges(enc_lens[0], dec_lens[0], lax.axis_size("grp"))
    rows = arrived.reshape(-1, LANES)
    worked = pl.pallas_call(
        attention_kernel,
        out_shape=jax.ShapeDtypeStruct(rows.shape, jnp.bfloat16),
        in_specs=[SMEM, SMEM, VMEM],
        out_specs=VMEM,
        scratch_shapes=[pltpu.VMEM((rows.shape[0] // 2, LANES), jnp.float32)],
        name="attention",
    )(starts, counts, rows)
    returned = lax.all_to_all(
        worked.reshape(arrived.shape), HEADS, split_axis=0, concat_axis=0, tiled=True
    )
    weight_sum = over_axes(jnp.sum(token_weight), DP_GRP)
    factor = row_count * lax.axis_size(DP) * lax.axis_size("grp") / weight_sum
    coef = jnp.stack([factor / math.sqrt(HD), jnp.where(side == 0, factor, 1.0)])
    result = pl.pallas_call(
        unpack_kernel,
        out_shape=jax.ShapeDtypeStruct(local_rows.shape, jnp.bfloat16),
        in_specs=[SMEM, SMEM, VMEM],
        out_specs=VMEM,
        name="unpack",
    )(coef, side.astype(jnp.int32).reshape(1), returned)
    return result[None]


def solution(mesh):
    torus = Mesh(
        mesh.devices.reshape(mesh.shape["side"], 2, 4, 2, mesh.shape["grp"]),
        ("side", "dp_0", "dp_1", "dp_2", "grp"),
    )
    placed = (P("side", None, DP_GRP, None), P(DP_GRP), P(DP, None), P(DP, None))
    return jax.shard_map(
        per_device,
        mesh=torus,
        in_specs=placed,
        out_specs=P("side", None, DP_GRP, None),
        check_vma=False,
    )
```
